32 devices in a mesh: outer: 4 (over y, core), inner: 8 (over z, x).
Axes of the slice: x: 2, y: 2, z: 4, core: 2. Of those that a mesh axis runs over, the one named last changes fastest.
Arguments:
- queries: bfloat16 [8192, 1024], P(('outer', 'inner')), may hold values from -100 to 100
- keys: bfloat16 [8192, 1024], P(('outer', 'inner')), may hold values from -6 to 6
- values: bfloat16 [8192, 1024], P(('outer', 'inner')), may hold values from -6 to 6
- modality: int32 [8192], P(('outer', 'inner')), may hold values 0 or 1
Outputs:
- attended: bfloat16 [8192, 1024], P(('outer', 'inner'))
The draws below stay inside these ranges and needn't reach their ends.
All inputs are finite; a program needn't handle non-finite values. No bound on the sum of `modality` on one device may be relied on, other than what follows from the above.
Results may differ from the reference program's by a relative error of at most 0.0034.
Values may be sent and summed in bfloat16 or wider, within the bound.
A program may use at most 128 MiB of HBM per device.

```python
import math
import jax
import jax.numpy as jnp
from jax import lax

HEADS = 8
HEAD_DIM = 128
BLOCK = 128
TOK_DEV = 256
DM = 1024
TOKENS = 8192
LEVELS = 5


def smooth_field(key):
    freq_key, phase_key = jax.random.split(key)
    device_total = TOKENS // TOK_DEV
    top_power = max(device_total.bit_length() - 1, 1)
    powers = jax.random.randint(freq_key, (DM,), 0, top_power)
    cycles = jnp.left_shift(jnp.ones((DM,), jnp.int32), powers)
    offsets = jax.random.uniform(phase_key, (DM,), jnp.float32, -math.pi, math.pi)
    places = jnp.arange(TOKENS, dtype=jnp.int32)
    turns = places[:, None] * cycles[None, :] % TOKENS
    return jnp.sin(turns.astype(jnp.float32) * (2.0 * math.pi / TOKENS) + offsets[None, :])


def base_keys(key):
    noise_key, smooth_key = jax.random.split(jax.random.fold_in(key, 11), 2)
    rough = jax.random.truncated_normal(noise_key, -4.0, 4.0, (TOKENS, DM), jnp.float32)
    return rough + smooth_field(smooth_key)


def draw_keys(key, part):
    return base_keys(key).astype(jnp.bfloat16)


def draw_queries(key, part):
    query_key = jax.random.fold_in(jax.random.fold_in(key, 23), 0)
    return jax.random.truncated_normal(query_key, -4.0, 4.0, (TOKENS, DM), jnp.float32).astype(jnp.bfloat16)


def draw_values(key, part):
    noise_key, smooth_key = jax.random.split(jax.random.fold_in(key, 37), 2)
    rough = jax.random.truncated_normal(noise_key, -4.0, 4.0, (TOKENS, DM), jnp.float32)
    return (rough + smooth_field(smooth_key)).astype(jnp.bfloat16)


def place_ends(entries, key, low, top_value):
    dims = entries.shape
    place = [jax.random.randint(jax.random.fold_in(key, axis), (), 0, dims[axis]) for axis in range(len(dims))]
    entries = entries.at[tuple(place)].set(low)
    longest = dims.index(max(dims))
    place[longest] = (place[longest] + 1) % dims[longest]
    return entries.at[tuple(place)].set(top_value)


def setup_inputs(seed: int = 0) -> dict:
    key_list = jax.random.split(jax.random.key(seed), 5)
    return {
        "queries": draw_queries(jax.random.fold_in(key_list[4], 71), 0),
        "keys": draw_keys(jax.random.fold_in(key_list[4], 71), 0),
        "values": draw_values(jax.random.fold_in(key_list[4], 71), 0),
        "modality": place_ends((jax.random.randint(key_list[3], (TOKENS,), 0, 3) < 1).astype(jnp.int32), jax.random.fold_in(key_list[3], 1), 0, 1),
    }


def coarsen(rows_in):
    paired = rows_in.astype(jnp.float32).reshape(rows_in.shape[0] // 2, 2, rows_in.shape[1])
    return (0.5 * (paired[:, 0] + paired[:, 1])).astype(jnp.bfloat16)


def reference(queries, keys, values, modality):
    key_levels = []
    value_levels = []
    key_now = keys
    value_now = values
    for level in range(LEVELS):
        key_now = coarsen(key_now)
        value_now = coarsen(value_now)
        key_levels.append(key_now)
        value_levels.append(value_now)
    key_pad = jnp.pad(keys, ((BLOCK, BLOCK), (0, 0)))
    value_pad = jnp.pad(values, ((BLOCK, BLOCK), (0, 0)))
    label_pad = jnp.pad(modality, (BLOCK, BLOCK), constant_values=-1)
    score_scale = HEAD_DIM ** -0.5
    columns = jnp.arange(3 * BLOCK, dtype=jnp.int32)
    middle = (columns >= BLOCK) & (columns < 2 * BLOCK)

    def one_block(block_index):
        start = (block_index * BLOCK).astype(jnp.int32)
        query_rows = lax.dynamic_slice_in_dim(queries, start, BLOCK, 0).astype(jnp.float32)
        query_rows = query_rows.reshape(BLOCK, HEADS, HEAD_DIM)
        key_parts = [lax.dynamic_slice_in_dim(key_pad, start, 3 * BLOCK, 0)]
        value_parts = [lax.dynamic_slice_in_dim(value_pad, start, 3 * BLOCK, 0)]
        key_labels = lax.dynamic_slice_in_dim(label_pad, start, 3 * BLOCK, 0)
        query_labels = lax.dynamic_slice_in_dim(modality, start, BLOCK, 0)
        near_mask = (key_labels[None, :] == query_labels[:, None]) | middle[None, :]
        allowed = jnp.concatenate([near_mask, jnp.ones((BLOCK, LEVELS * BLOCK), bool)], axis=1)
        for level in range(LEVELS):
            node_index = block_index // (2 ** (level + 1))
            sibling = (node_index + 1 - 2 * (node_index % 2)).astype(jnp.int32)
            key_parts.append(lax.dynamic_slice_in_dim(key_levels[level], sibling * BLOCK, BLOCK, 0))
            value_parts.append(lax.dynamic_slice_in_dim(value_levels[level], sibling * BLOCK, BLOCK, 0))
        all_keys = jnp.concatenate(key_parts, axis=0).astype(jnp.float32).reshape(-1, HEADS, HEAD_DIM)
        all_values = jnp.concatenate(value_parts, axis=0).astype(jnp.float32).reshape(-1, HEADS, HEAD_DIM)
        logits = jnp.einsum("qhd,khd->hqk", query_rows, all_keys) * score_scale
        logits = jnp.where(allowed[None], logits, -jnp.inf)
        row_top = jnp.max(logits, axis=2, keepdims=True)
        weights = jnp.exp(logits - row_top)
        denominator = jnp.sum(weights, axis=2)
        rounded = lax.optimization_barrier(weights.astype(jnp.bfloat16)).astype(jnp.float32)
        numerator = jnp.einsum("hqk,khd->qhd", rounded, all_values)
        result = numerator / denominator.T[:, :, None]
        return result.reshape(BLOCK, HEADS * HEAD_DIM).astype(jnp.bfloat16)

    block_ids = jnp.arange(TOKENS // BLOCK, dtype=jnp.int32)
    outputs = lax.map(one_block, block_ids, batch_size=16)
    return outputs.reshape(TOKENS, HEADS * HEAD_DIM)
```

```python
import functools
import math

import jax
import jax.numpy as jnp
from jax import lax
from jax.experimental import pallas as pl
from jax.experimental.pallas import tpu as pltpu
from jax.sharding import PartitionSpec as P

HEAD_DIM = 128
BLOCK = 128
AXES = ("outer", "inner")
MESH = pl.DeviceIdType.MESH
F32 = jnp.float32
BF16 = jnp.bfloat16
HELPERS = {2: 1, 4: 3}


def pair_means(rows):
    half = rows.shape[0] // 2
    r = lax.broadcasted_iota(jnp.int32, (half, rows.shape[0]), 0)
    c = lax.broadcasted_iota(jnp.int32, (half, rows.shape[0]), 1)
    mix = jnp.where(c // 2 == r, 0.5, 0.0).astype(BF16)
    return jnp.dot(mix, rows, preferred_element_type=F32).astype(BF16)


def kernel(
    levels, inner, q_ref, k_ref, v_ref, mod_ref, out_ref,
    node, far, near, near_mod, bias_own, bias_near, m_ref, l_ref, acc_ref,
    far_send, far_recv, near_send, near_recv,
):
    rows = q_ref.shape[0]
    heads = q_ref.shape[1] // HEAD_DIM
    count = 2**levels
    me = lax.axis_index("outer") * inner + lax.axis_index("inner")
    scale = HEAD_DIM**-0.5 * math.log2(math.e)
    own = (k_ref, v_ref)

    def place(d):
        return (d // inner, d % inner)

    def bit(b):
        return me // 2**b % 2

    def flip(b):
        return me + 2**b * (1 - 2 * bit(b))

    after = (me + 1) % count
    before = (me + count - 1) % count

    @pl.when(me == 0)
    def _():
        near[0] = jnp.zeros(near.shape[1:], BF16)
        near_mod[0] = jnp.full(near_mod.shape[1:], -1, jnp.int32)

    @pl.when(me == count - 1)
    def _():
        near[1] = jnp.zeros(near.shape[1:], BF16)
        near_mod[1] = jnp.full(near_mod.shape[1:], -1, jnp.int32)

    for part in range(2):
        node[0, part] = pair_means(own[part][...])

    barrier = pltpu.get_barrier_semaphore()
    for target in [flip(b) for b in range(levels)] + [after, before]:
        pl.semaphore_signal(barrier, inc=1, device_id=place(target), device_id_type=MESH)
    pl.semaphore_wait(barrier, levels + 2)

    def remote(src, dst, send, recv, target):
        return pltpu.make_async_remote_copy(
            src_ref=src, dst_ref=dst, send_sem=send, recv_sem=recv,
            device_id=place(target), device_id_type=MESH,
        )

    def half_rows(h):
        return pl.ds(pl.multiple_of(bit(h) * (BLOCK // 2), BLOCK // 2), BLOCK // 2)

    def level_copy(b, part):
        sems = (far_send.at[b, part, 0], far_recv.at[b, part, 0])
        if b in HELPERS:
            span = half_rows(HELPERS[b])
            return remote(node.at[b, part, span], far.at[b, part, span], *sems, flip(b))
        return remote(node.at[b, part], far.at[b, part], *sems, flip(b))

    def share_copy(b, part):
        span = half_rows(HELPERS[b])
        view = far.at[b, part, span]
        return remote(view, view, far_send.at[b, part, 1], far_recv.at[b, part, 1], flip(HELPERS[b]))

    def near_copies(side):
        target = after if side == 0 else before
        start = rows - BLOCK if side == 0 else 0
        copies = [
            remote(own[part].at[pl.ds(start, BLOCK)], near.at[side, part],
                   near_send.at[side, part], near_recv.at[side, part], target)
            for part in range(2)
        ]
        copies.append(
            remote(mod_ref.at[start // BLOCK], near_mod.at[side],
                   near_send.at[side, 2], near_recv.at[side, 2], target)
        )
        return copies

    def start_near(side):
        for copy in near_copies(side):
            copy.start()

    for part in range(2):
        level_copy(0, part).start()
    pl.when(bit(0) == 0)(lambda: start_near(0))
    pl.when(bit(0) == 1)(lambda: start_near(1))

    def label_rows(i):
        return jnp.broadcast_to(mod_ref[i].astype(F32), (BLOCK, BLOCK))

    labels = [label_rows(0), label_rows(1)]
    columns = [jnp.transpose(x) for x in labels]
    zero = jnp.zeros((BLOCK, BLOCK), F32)
    for i in range(2):
        for j in range(2):
            value = zero if i == j else jnp.where(labels[j] == columns[i], 0.0, -jnp.inf)
            bias_own[i * BLOCK : (i + 1) * BLOCK, j * BLOCK : (j + 1) * BLOCK] = value

    def head_cols(h):
        return pl.ds(pl.multiple_of(h * HEAD_DIM, HEAD_DIM), HEAD_DIM)

    def score(q, k):
        return lax.dot_general(q, k, (((1,), (1,)), ((), ())), preferred_element_type=F32) * scale

    def first(h):
        cols = head_cols(h)
        s = score(q_ref[:, cols], k_ref[:, cols]) + bias_own[...]
        m = jnp.broadcast_to(jnp.max(s, axis=1, keepdims=True), (rows, BLOCK))
        p0 = jnp.exp2(s[:, :BLOCK] - m)
        p1 = jnp.exp2(s[:, BLOCK:] - m)
        m_ref[h] = m
        l_ref[h] = p0 + p1
        p = jnp.concatenate([p0.astype(BF16), p1.astype(BF16)], axis=1)
        acc_ref[h] = jnp.dot(p, v_ref[:, cols], preferred_element_type=F32)

    def merged(h, span, k, v, bias):
        cols = head_cols(h)
        s = score(q_ref[span, cols], k[:, cols])
        if bias is not None:
            s = s + bias[...]
        m_old = m_ref[h, span]
        m = jnp.maximum(m_old, jnp.max(s, axis=1, keepdims=True))
        p = jnp.exp2(s - m)
        a = jnp.exp2(m_old - m)
        l = l_ref[h, span] * a + p
        acc = acc_ref[h, span] * a + jnp.dot(p.astype(BF16), v[:, cols], preferred_element_type=F32)
        return m, l, acc

    def update(h, span, k, v, bias=None):
        m, l, acc = merged(h, span, k, v, bias)
        m_ref[h, span] = m
        l_ref[h, span] = l
        acc_ref[h, span] = acc

    def every_head(body):
        def step(h, carry):
            body(h)
            return carry

        lax.fori_loop(0, heads, step, 0, unroll=2)

    everything = pl.ds(0, rows)

    def near_update(side):
        i = side
        other = jnp.broadcast_to(near_mod[side].astype(F32), (BLOCK, BLOCK))
        mine = jnp.transpose(label_rows(i))
        bias_near[side] = jnp.where(other == mine, 0.0, -jnp.inf)
        every_head(
            lambda h: update(h, pl.ds(i * BLOCK, BLOCK), near.at[side, 0], near.at[side, 1], bias_near.at[side])
        )

    def wait_near(side):
        has = me > 0 if side == 0 else me < count - 1

        @pl.when(has)
        def _():
            for copy in near_copies(side):
                copy.wait_recv()

    def far_head(b):
        def body(h):
            update(h, everything, far.at[b, 0], far.at[b, 1])

        return body

    def last_head(h):
        m, l, acc = merged(h, everything, far.at[levels - 1, 0], far.at[levels - 1, 1], None)
        total = jnp.sum(l, axis=1, keepdims=True)
        out_ref[:, head_cols(h)] = (acc / total).astype(BF16)

    every_head(first)
    for b in range(levels):
        if b in HELPERS:
            for part in range(2):
                level_copy(b, part).wait_recv()
                share_copy(b, part).start()
        if b == levels - 1:
            for side in range(2):
                wait_near(side)
                near_update(side)
        for part in range(2):
            if b in HELPERS:
                share_copy(b, part).wait_recv()
            else:
                level_copy(b, part).wait_recv()
            if b + 1 < levels:
                for source, upper in ((node, bit(b)), (far, 1 - bit(b))):
                    span = pl.ds(pl.multiple_of(upper * (BLOCK // 2), BLOCK // 2), BLOCK // 2)
                    node[b + 1, part, span, :] = pair_means(source[b, part])
                level_copy(b + 1, part).start()
        if b == 0:
            pl.when((bit(0) == 0) & (me > 0))(lambda: start_near(1))
            pl.when((bit(0) == 1) & (me < count - 1))(lambda: start_near(0))
        if b < levels - 1:
            every_head(far_head(b))
    every_head(last_head)

    for b in range(levels):
        for part in range(2):
            level_copy(b, part).wait_send()
            if b in HELPERS:
                share_copy(b, part).wait_send()
    for side, has in ((0, me < count - 1), (1, me > 0)):

        @pl.when(has)
        def _(side=side):
            for copy in near_copies(side):
                copy.wait_send()


def shards(levels, inner, queries, keys, values, modality):
    rows, width = queries.shape
    heads = width // HEAD_DIM
    labels = modality.reshape(rows // BLOCK, 1, BLOCK)
    vmem = pl.BlockSpec(memory_space=pltpu.VMEM)
    state = pltpu.VMEM((heads, rows, HEAD_DIM), F32)
    return pl.pallas_call(
        functools.partial(kernel, levels, inner),
        out_shape=jax.ShapeDtypeStruct((rows, width), BF16),
        in_specs=[vmem] * 4,
        out_specs=vmem,
        scratch_shapes=[
            pltpu.VMEM((levels, 2, BLOCK, width), BF16),
            pltpu.VMEM((levels, 2, BLOCK, width), BF16),
            pltpu.VMEM((2, 2, BLOCK, width), BF16),
            pltpu.VMEM((2, 1, BLOCK), jnp.int32),
            pltpu.VMEM((rows, 2 * BLOCK), F32),
            pltpu.VMEM((2, BLOCK, BLOCK), F32),
            state,
            state,
            state,
            pltpu.SemaphoreType.DMA((levels, 2, 2)),
            pltpu.SemaphoreType.DMA((levels, 2, 2)),
            pltpu.SemaphoreType.DMA((2, 3)),
            pltpu.SemaphoreType.DMA((2, 3)),
        ],
        compiler_params=pltpu.CompilerParams(
            collective_id=0, has_side_effects=True, vmem_limit_bytes=56 * 2**20
        ),
    )(queries, keys, values, labels)


def solution(mesh):
    outer, inner = mesh.shape["outer"], mesh.shape["inner"]
    levels = (outer * inner).bit_length() - 1
    rows = P(AXES, None)
    return jax.shard_map(
        functools.partial(shards, levels, inner),
        mesh=mesh,
        in_specs=(rows, rows, rows, P(AXES)),
        out_specs=rows,
        check_vma=False,
    )
```

```python
import functools
import math

import jax
import jax.numpy as jnp
from jax import lax
from jax.experimental import pallas as pl
from jax.experimental.pallas import tpu as pltpu
from jax.sharding import PartitionSpec as P

HEAD_DIM = 128
BLOCK = 128
AXES = ("outer", "inner")
MESH = pl.DeviceIdType.MESH
F32 = jnp.float32
BF16 = jnp.bfloat16
SHARED = (2, 4)
SPLIT = 1


def pair_means(rows):
    half = rows.shape[0] // 2
    r = lax.broadcasted_iota(jnp.int32, (half, rows.shape[0]), 0)
    c = lax.broadcasted_iota(jnp.int32, (half, rows.shape[0]), 1)
    mix = jnp.where(c // 2 == r, 0.5, 0.0).astype(BF16)
    return jnp.dot(mix, rows, preferred_element_type=F32).astype(BF16)


def kernel(
    levels, inner, q_ref, k_ref, v_ref, mod_ref, out_ref,
    node, far, near, near_mod, bias_own, bias_near, m_ref, l_ref, acc_ref,
    far_send, far_recv, near_send, near_recv,
):
    rows = q_ref.shape[0]
    heads = q_ref.shape[1] // HEAD_DIM
    count = 2**levels
    me = lax.axis_index("outer") * inner + lax.axis_index("inner")
    scale = HEAD_DIM**-0.5 * math.log2(math.e)
    own = (k_ref, v_ref)

    def place(d):
        return (d // inner, d % inner)

    def bit(b):
        return me // 2**b % 2

    def flip(b):
        return me + 2**b * (1 - 2 * bit(b))

    after = (me + 1) % count
    before = (me + count - 1) % count

    @pl.when(me == 0)
    def _():
        near[0] = jnp.zeros(near.shape[1:], BF16)
        near_mod[0] = jnp.full(near_mod.shape[1:], -1, jnp.int32)

    @pl.when(me == count - 1)
    def _():
        near[1] = jnp.zeros(near.shape[1:], BF16)
        near_mod[1] = jnp.full(near_mod.shape[1:], -1, jnp.int32)

    for part in range(2):
        node[0, part] = pair_means(own[part][...])

    barrier = pltpu.get_barrier_semaphore()
    for target in [flip(b) for b in range(levels)] + [after, before]:
        pl.semaphore_signal(barrier, inc=1, device_id=place(target), device_id_type=MESH)
    pl.semaphore_wait(barrier, levels + 2)

    def remote(src, dst, send, recv, target):
        return pltpu.make_async_remote_copy(
            src_ref=src, dst_ref=dst, send_sem=send, recv_sem=recv,
            device_id=place(target), device_id_type=MESH,
        )

    def half_rows(upper):
        return pl.ds(pl.multiple_of(upper * (BLOCK // 2), BLOCK // 2), BLOCK // 2)

    def whole_copy(b, part):
        return remote(node.at[b, part], far.at[b, part], far_send.at[b, part, 0], far_recv.at[b, part, 0], flip(b))

    def half_copy(b, part, slot):
        span = half_rows(bit(b - 1) if slot == 0 else 1 - bit(b - 1))
        return remote(node.at[b, part, span], far.at[b, part, span],
                      far_send.at[b, part, slot], far_recv.at[b, part, slot], flip(b))

    def share_copy(b, part):
        view = far.at[b, part, half_rows(bit(b - 1))]
        return remote(view, view, far_send.at[b, part, 1], far_recv.at[b, part, 1], flip(b - 1))

    def level_copies(b, part):
        if b in SHARED:
            return [half_copy(b, part, 0), share_copy(b, part)]
        if b == SPLIT:
            return [half_copy(b, part, 0), half_copy(b, part, 1)]
        return [whole_copy(b, part)]

    def own_ready(b, part):
        if b < levels:
            node[b, part, half_rows(bit(b - 1)), :] = pair_means(node[b - 1, part])
            if b in SHARED or b == SPLIT:
                half_copy(b, part, 0).start()

    def far_ready(b, part):
        if b < levels:
            if b not in SHARED or b + 1 < levels:
                node[b, part, half_rows(1 - bit(b - 1)), :] = pair_means(far[b - 1, part])
            if b == SPLIT:
                half_copy(b, part, 1).start()
            elif b not in SHARED:
                whole_copy(b, part).start()
            own_ready(b + 1, part)

    def wait_first(b):
        if b in SHARED:
            for part in range(2):
                half_copy(b, part, 0).wait_recv()
                share_copy(b, part).start()

    def wait_level(b):
        for part in range(2):
            for copy in level_copies(b, part)[1 if b in SHARED else 0 :]:
                copy.wait_recv()
            far_ready(b + 1, part)

    def near_copies(side):
        target = after if side == 0 else before
        start = rows - BLOCK if side == 0 else 0
        copies = [
            remote(own[part].at[pl.ds(start, BLOCK)], near.at[side, part],
                   near_send.at[side, part], near_recv.at[side, part], target)
            for part in range(2)
        ]
        copies.append(
            remote(mod_ref.at[start // BLOCK], near_mod.at[side],
                   near_send.at[side, 2], near_recv.at[side, 2], target)
        )
        return copies

    def start_near(side):
        for copy in near_copies(side):
            copy.start()

    for part in range(2):
        whole_copy(0, part).start()
    for part in range(2):
        own_ready(1, part)
    pl.when(bit(0) == 0)(lambda: start_near(0))
    pl.when(bit(0) == 1)(lambda: start_near(1))

    def label_rows(i):
        return jnp.broadcast_to(mod_ref[i].astype(F32), (BLOCK, BLOCK))

    labels = [label_rows(0), label_rows(1)]
    columns = [jnp.transpose(x) for x in labels]
    zero = jnp.zeros((BLOCK, BLOCK), F32)
    for i in range(2):
        for j in range(2):
            value = zero if i == j else jnp.where(labels[j] == columns[i], 0.0, -jnp.inf)
            bias_own[i * BLOCK : (i + 1) * BLOCK, j * BLOCK : (j + 1) * BLOCK] = value

    def head_cols(h):
        return pl.ds(pl.multiple_of(h * HEAD_DIM, HEAD_DIM), HEAD_DIM)

    def score(q, k):
        return lax.dot_general(q, k, (((1,), (1,)), ((), ())), preferred_element_type=F32) * scale

    def first(h):
        cols = head_cols(h)
        s = score(q_ref[:, cols], k_ref[:, cols]) + bias_own[...]
        m = jnp.broadcast_to(jnp.max(s, axis=1, keepdims=True), (rows, BLOCK))
        p0 = jnp.exp2(s[:, :BLOCK] - m)
        p1 = jnp.exp2(s[:, BLOCK:] - m)
        m_ref[h] = m
        l_ref[h] = p0 + p1
        p = jnp.concatenate([p0.astype(BF16), p1.astype(BF16)], axis=1)
        acc_ref[h] = jnp.dot(p, v_ref[:, cols], preferred_element_type=F32)

    def merged(h, span, k, v, bias):
        cols = head_cols(h)
        s = score(q_ref[span, cols], k[:, cols])
        if bias is not None:
            s = s + bias[...]
        m_old = m_ref[h, span]
        m = jnp.maximum(m_old, jnp.max(s, axis=1, keepdims=True))
        p = jnp.exp2(s - m)
        a = jnp.exp2(m_old - m)
        l = l_ref[h, span] * a + p
        acc = acc_ref[h, span] * a + jnp.dot(p.astype(BF16), v[:, cols], preferred_element_type=F32)
        return m, l, acc

    def update(h, span, k, v, bias=None):
        m, l, acc = merged(h, span, k, v, bias)
        m_ref[h, span] = m
        l_ref[h, span] = l
        acc_ref[h, span] = acc

    def every_head(body):
        def step(h, carry):
            body(h)
            return carry

        lax.fori_loop(0, heads, step, 0, unroll=8)

    everything = pl.ds(0, rows)

    def near_update(side):
        i = side
        block = pl.ds(pl.multiple_of(side * BLOCK, BLOCK), BLOCK)
        other = jnp.broadcast_to(near_mod[side].astype(F32), (BLOCK, BLOCK))
        mine = jnp.transpose(label_rows(i))
        bias_near[side] = jnp.where(other == mine, 0.0, -jnp.inf)
        every_head(
            lambda h: update(h, block, near.at[side, 0], near.at[side, 1], bias_near.at[side])
        )

    def wait_pair(turn):
        for side in range(2):
            has = me > 0 if side == 0 else me < count - 1

            @pl.when(has & (bit(0) == (1 - side if turn == 0 else side)))
            def _():
                for copy in near_copies(side):
                    copy.wait_recv()

    def far_head(b):
        def body(h):
            update(h, everything, far.at[b, 0], far.at[b, 1])

        return body

    def last_head(h):
        m, l, acc = merged(h, everything, far.at[levels - 1, 0], far.at[levels - 1, 1], None)
        total = jnp.sum(l, axis=1, keepdims=True)
        out_ref[:, head_cols(h)] = (acc / total).astype(BF16)

    every_head(first)
    for b in range(levels):
        wait_first(b)
        if b == levels - 1:
            wait_pair(1)
            near_update(bit(0))
        wait_level(b)
        if b == 0:
            pl.when((bit(0) == 0) & (me > 0))(lambda: start_near(1))
            pl.when((bit(0) == 1) & (me < count - 1))(lambda: start_near(0))
        if b == 2:
            wait_pair(0)
            near_update(1 - bit(0))
        if b < levels - 1:
            every_head(far_head(b))
    every_head(last_head)

    for b in range(levels):
        for part in range(2):
            for copy in level_copies(b, part):
                copy.wait_send()
    for side, has in ((0, me < count - 1), (1, me > 0)):

        @pl.when(has)
        def _(side=side):
            for copy in near_copies(side):
                copy.wait_send()


def shards(levels, inner, queries, keys, values, modality):
    rows, width = queries.shape
    heads = width // HEAD_DIM
    labels = modality.reshape(rows // BLOCK, 1, BLOCK)
    vmem = pl.BlockSpec(memory_space=pltpu.VMEM)
    state = pltpu.VMEM((heads, rows, HEAD_DIM), F32)
    return pl.pallas_call(
        functools.partial(kernel, levels, inner),
        out_shape=jax.ShapeDtypeStruct((rows, width), BF16),
        in_specs=[vmem] * 4,
        out_specs=vmem,
        scratch_shapes=[
            pltpu.VMEM((levels, 2, BLOCK, width), BF16),
            pltpu.VMEM((levels, 2, BLOCK, width), BF16),
            pltpu.VMEM((2, 2, BLOCK, width), BF16),
            pltpu.VMEM((2, 1, BLOCK), jnp.int32),
            pltpu.VMEM((rows, 2 * BLOCK), F32),
            pltpu.VMEM((2, BLOCK, BLOCK), F32),
            state,
            state,
            state,
            pltpu.SemaphoreType.DMA((levels, 2, 2)),
            pltpu.SemaphoreType.DMA((levels, 2, 2)),
            pltpu.SemaphoreType.DMA((2, 3)),
            pltpu.SemaphoreType.DMA((2, 3)),
        ],
        compiler_params=pltpu.CompilerParams(
            collective_id=0, has_side_effects=True, vmem_limit_bytes=56 * 2**20
        ),
    )(queries, keys, values, labels)


def solution(mesh):
    outer, inner = mesh.shape["outer"], mesh.shape["inner"]
    levels = (outer * inner).bit_length() - 1
    rows = P(AXES, None)
    return jax.shard_map(
        functools.partial(shards, levels, inner),
        mesh=mesh,
        in_specs=(rows, rows, rows, P(AXES)),
        out_specs=rows,
        check_vma=False,
    )
```

```python
import functools
import math

import jax
import jax.numpy as jnp
from jax import lax
from jax.experimental import pallas as pl
from jax.experimental.pallas import tpu as pltpu
from jax.sharding import PartitionSpec as P

HEAD_DIM = 128
BLOCK = 128
AXES = ("outer", "inner")
MESH = pl.DeviceIdType.MESH
F32 = jnp.float32
BF16 = jnp.bfloat16
SHARED = (2, 4)
SPLIT = 1


def pair_means(rows):
    half = rows.shape[0] // 2
    r = lax.broadcasted_iota(jnp.int32, (half, rows.shape[0]), 0)
    c = lax.broadcasted_iota(jnp.int32, (half, rows.shape[0]), 1)
    mix = jnp.where(c // 2 == r, 0.5, 0.0).astype(BF16)
    return jnp.dot(mix, rows, preferred_element_type=F32).astype(BF16)


def kernel(
    levels, inner, q_ref, k_ref, v_ref, mod_ref, out_ref,
    node, far, near, near_mod, bias_own, bias_near, m_ref, l_ref, acc_ref,
    far_send, far_recv, near_send, near_recv, relay, relay_send, relay_recv,
):
    rows = q_ref.shape[0]
    heads = q_ref.shape[1] // HEAD_DIM
    count = 2**levels
    me = lax.axis_index("outer") * inner + lax.axis_index("inner")
    scale = HEAD_DIM**-0.5 * math.log2(math.e)
    own = (k_ref, v_ref)

    def place(d):
        return (d // inner, d % inner)

    def bit(b):
        return me // 2**b % 2

    def flip(b):
        return me + 2**b * (1 - 2 * bit(b))

    after = (me + 1) % count
    before = (me + count - 1) % count
    two_after = (me + 2) % count
    two_before = (me + count - 2) % count

    @pl.when(me == 0)
    def _():
        near[0] = jnp.zeros(near.shape[1:], BF16)
        near_mod[0] = jnp.full(near_mod.shape[1:], -1, jnp.int32)

    @pl.when(me == count - 1)
    def _():
        near[1] = jnp.zeros(near.shape[1:], BF16)
        near_mod[1] = jnp.full(near_mod.shape[1:], -1, jnp.int32)

    for part in range(2):
        node[0, part] = pair_means(own[part][...])

    barrier = pltpu.get_barrier_semaphore()
    for target in [flip(b) for b in range(levels)] + [after, before, two_after, two_before]:
        pl.semaphore_signal(barrier, inc=1, device_id=place(target), device_id_type=MESH)
    pl.semaphore_wait(barrier, levels + 4)

    def remote(src, dst, send, recv, target):
        return pltpu.make_async_remote_copy(
            src_ref=src, dst_ref=dst, send_sem=send, recv_sem=recv,
            device_id=place(target), device_id_type=MESH,
        )

    def half_rows(upper):
        return pl.ds(pl.multiple_of(upper * (BLOCK // 2), BLOCK // 2), BLOCK // 2)

    def whole_copy(b, part):
        return remote(node.at[b, part], far.at[b, part], far_send.at[b, part, 0], far_recv.at[b, part, 0], flip(b))

    def half_copy(b, part, slot):
        span = half_rows(bit(b - 1) if slot == 0 else 1 - bit(b - 1))
        return remote(node.at[b, part, span], far.at[b, part, span],
                      far_send.at[b, part, slot], far_recv.at[b, part, slot], flip(b))

    def share_copy(b, part):
        view = far.at[b, part, half_rows(bit(b - 1))]
        return remote(view, view, far_send.at[b, part, 1], far_recv.at[b, part, 1], flip(b - 1))

    def level_copies(b, part):
        if b in SHARED:
            return [half_copy(b, part, 0), share_copy(b, part)]
        if b == SPLIT:
            return [half_copy(b, part, 0), half_copy(b, part, 1)]
        return [whole_copy(b, part)]

    def own_ready(b, part):
        if b < levels:
            node[b, part, half_rows(bit(b - 1)), :] = pair_means(node[b - 1, part])
            if b in SHARED or b == SPLIT:
                half_copy(b, part, 0).start()

    def far_ready(b, part):
        if b < levels:
            if b not in SHARED or b + 1 < levels:
                node[b, part, half_rows(1 - bit(b - 1)), :] = pair_means(far[b - 1, part])
            if b == SPLIT:
                half_copy(b, part, 1).start()
            elif b not in SHARED:
                whole_copy(b, part).start()
            own_ready(b + 1, part)

    def wait_first(b):
        if b in SHARED:
            for part in range(2):
                half_copy(b, part, 0).wait_recv()
                share_copy(b, part).start()

    def wait_level(b):
        for part in range(2):
            for copy in level_copies(b, part)[1 if b in SHARED else 0 :]:
                copy.wait_recv()
            far_ready(b + 1, part)

    def near_copies(side):
        target = after if side == 0 else before
        start = rows - BLOCK if side == 0 else 0
        copies = [
            remote(own[part].at[pl.ds(start, BLOCK)], near.at[side, part],
                   near_send.at[side, part], near_recv.at[side, part], target)
            for part in range(2)
        ]
        copies.append(
            remote(mod_ref.at[start // BLOCK], near_mod.at[side],
                   near_send.at[side, 2], near_recv.at[side, 2], target)
        )
        return copies

    def start_near(side):
        for copy in near_copies(side):
            copy.start()

    def relay_in(side):
        start = rows - BLOCK if side == 0 else 0
        return remote(v_ref.at[pl.ds(start, BLOCK)], relay, near_send.at[side, 1], relay_recv,
                      two_after if side == 0 else two_before)

    def start_cross(side):
        near_copies(side)[0].start()
        near_copies(side)[2].start()

    def relay_out(side):
        return remote(relay, near.at[side, 1], relay_send, near_recv.at[side, 1], flip(0))

    def on_relay(action):
        pl.when((bit(0) == 0) & (me + 2 < count))(lambda: action(1))
        pl.when((bit(0) == 1) & (me > 2))(lambda: action(0))

    def hand_over(side):
        relay_in(side).wait_recv()
        relay_out(side).start()

    for part in range(2):
        whole_copy(0, part).start()
    for part in range(2):
        own_ready(1, part)
    pl.when((bit(0) == 0) & (me > 0))(lambda: relay_in(1).start())
    pl.when((bit(0) == 1) & (me < count - 1))(lambda: relay_in(0).start())
    pl.when(bit(0) == 0)(lambda: start_near(0))
    pl.when(bit(0) == 1)(lambda: start_near(1))

    def label_rows(i):
        return jnp.broadcast_to(mod_ref[i].astype(F32), (BLOCK, BLOCK))

    labels = [label_rows(0), label_rows(1)]
    columns = [jnp.transpose(x) for x in labels]
    zero = jnp.zeros((BLOCK, BLOCK), F32)
    for i in range(2):
        for j in range(2):
            value = zero if i == j else jnp.where(labels[j] == columns[i], 0.0, -jnp.inf)
            bias_own[i * BLOCK : (i + 1) * BLOCK, j * BLOCK : (j + 1) * BLOCK] = value

    def head_cols(h):
        return pl.ds(pl.multiple_of(h * HEAD_DIM, HEAD_DIM), HEAD_DIM)

    def score(q, k):
        return lax.dot_general(q, k, (((1,), (1,)), ((), ())), preferred_element_type=F32) * scale

    def first(h):
        cols = head_cols(h)
        s = score(q_ref[:, cols], k_ref[:, cols]) + bias_own[...]
        m = jnp.broadcast_to(jnp.max(s, axis=1, keepdims=True), (rows, BLOCK))
        p0 = jnp.exp2(s[:, :BLOCK] - m)
        p1 = jnp.exp2(s[:, BLOCK:] - m)
        m_ref[h] = m
        l_ref[h] = p0 + p1
        p = jnp.concatenate([p0.astype(BF16), p1.astype(BF16)], axis=1)
        acc_ref[h] = jnp.dot(p, v_ref[:, cols], preferred_element_type=F32)

    def merged(h, span, k, v, bias):
        cols = head_cols(h)
        s = score(q_ref[span, cols], k[:, cols])
        if bias is not None:
            s = s + bias[...]
        m_old = m_ref[h, span]
        m = jnp.maximum(m_old, jnp.max(s, axis=1, keepdims=True))
        p = jnp.exp2(s - m)
        a = jnp.exp2(m_old - m)
        l = l_ref[h, span] * a + p
        acc = acc_ref[h, span] * a + jnp.dot(p.astype(BF16), v[:, cols], preferred_element_type=F32)
        return m, l, acc

    def update(h, span, k, v, bias=None):
        m, l, acc = merged(h, span, k, v, bias)
        m_ref[h, span] = m
        l_ref[h, span] = l
        acc_ref[h, span] = acc

    def every_head(body):
        def step(h, carry):
            body(h)
            return carry

        lax.fori_loop(0, heads, step, 0, unroll=8)

    everything = pl.ds(0, rows)

    def near_update(side):
        i = side
        block = pl.ds(pl.multiple_of(side * BLOCK, BLOCK), BLOCK)
        other = jnp.broadcast_to(near_mod[side].astype(F32), (BLOCK, BLOCK))
        mine = jnp.transpose(label_rows(i))
        bias_near[side] = jnp.where(other == mine, 0.0, -jnp.inf)
        every_head(
            lambda h: update(h, block, near.at[side, 0], near.at[side, 1], bias_near.at[side])
        )

    def wait_pair(turn):
        for side in range(2):
            has = me > 0 if side == 0 else me < count - 1

            @pl.when(has & (bit(0) == (1 - side if turn == 0 else side)))
            def _():
                for copy in near_copies(side):
                    copy.wait_recv()

    def far_head(b):
        def body(h):
            update(h, everything, far.at[b, 0], far.at[b, 1])

        return body

    def last_head(h):
        m, l, acc = merged(h, everything, far.at[levels - 1, 0], far.at[levels - 1, 1], None)
        total = jnp.sum(l, axis=1, keepdims=True)
        out_ref[:, head_cols(h)] = (acc / total).astype(BF16)

    every_head(first)
    for b in range(levels):
        wait_first(b)
        if b == 1:
            on_relay(hand_over)
        if b == levels - 1:
            wait_pair(1)
            near_update(bit(0))
        wait_level(b)
        if b == 0:
            pl.when((bit(0) == 0) & (me > 0))(lambda: start_cross(1))
            pl.when((bit(0) == 1) & (me < count - 1))(lambda: start_cross(0))
        if b == 2:
            wait_pair(0)
            near_update(1 - bit(0))
        if b < levels - 1:
            every_head(far_head(b))
    every_head(last_head)

    on_relay(lambda side: relay_out(side).wait_send())
    for b in range(levels):
        for part in range(2):
            for copy in level_copies(b, part):
                copy.wait_send()
    for side, has in ((0, me < count - 1), (1, me > 0)):

        @pl.when(has)
        def _(side=side):
            for copy in near_copies(side):
                copy.wait_send()


def shards(levels, inner, queries, keys, values, modality):
    rows, width = queries.shape
    heads = width // HEAD_DIM
    labels = modality.reshape(rows // BLOCK, 1, BLOCK)
    vmem = pl.BlockSpec(memory_space=pltpu.VMEM)
    state = pltpu.VMEM((heads, rows, HEAD_DIM), F32)
    return pl.pallas_call(
        functools.partial(kernel, levels, inner),
        out_shape=jax.ShapeDtypeStruct((rows, width), BF16),
        in_specs=[vmem] * 4,
        out_specs=vmem,
        scratch_shapes=[
            pltpu.VMEM((levels, 2, BLOCK, width), BF16),
            pltpu.VMEM((levels, 2, BLOCK, width), BF16),
            pltpu.VMEM((2, 2, BLOCK, width), BF16),
            pltpu.VMEM((2, 1, BLOCK), jnp.int32),
            pltpu.VMEM((rows, 2 * BLOCK), F32),
            pltpu.VMEM((2, BLOCK, BLOCK), F32),
            state,
            state,
            state,
            pltpu.SemaphoreType.DMA((levels, 2, 2)),
            pltpu.SemaphoreType.DMA((levels, 2, 2)),
            pltpu.SemaphoreType.DMA((2, 3)),
            pltpu.SemaphoreType.DMA((2, 3)),
            pltpu.VMEM((BLOCK, width), BF16),
            pltpu.SemaphoreType.DMA(()),
            pltpu.SemaphoreType.DMA(()),
        ],
        compiler_params=pltpu.CompilerParams(
            collective_id=0, has_side_effects=True, vmem_limit_bytes=56 * 2**20
        ),
    )(queries, keys, values, labels)


def solution(mesh):
    outer, inner = mesh.shape["outer"], mesh.shape["inner"]
    levels = (outer * inner).bit_length() - 1
    rows = P(AXES, None)
    return jax.shard_map(
        functools.partial(shards, levels, inner),
        mesh=mesh,
        in_specs=(rows, rows, rows, P(AXES)),
        out_specs=rows,
        check_vma=False,
    )
```
